32 devices in a mesh: vert: 32 (over z, y, x, core).
Axes of the slice: x: 2, y: 2, z: 4, core: 2. Of those that a mesh axis runs over, the one named last changes fastest.
Arguments:
- features: bfloat16 [32768, 512], P('vert'), may hold values from -6 to 6
- send_rows: int32 [32, 32, 4], P('vert'), may hold values from 0 to 1023
- mirror_count: int32 [32, 32], P('vert'), may hold values from 1 to 4, as said below
- tile_coord: int32 [32, 2, 128], P('vert'), may hold values from 0 to 8
- tile_mask: int32 [32, 128, 128, 128], P('vert'), may hold values 0 or 1
- tile_count: int32 [32], P('vert'), may hold values from 32 to 128, as said below
- w_self1: bfloat16 [512, 512], replicated, may hold values from -0.25 to 0.25
- w_neigh1: bfloat16 [512, 512], replicated, may hold values from -1 to 1
- bias1: bfloat16 [512], replicated, may hold values from -3 to 3
- w_self2: bfloat16 [512, 512], replicated, may hold values from -0.25 to 0.25
- w_neigh2: bfloat16 [512, 512], replicated, may hold values from -1 to 1
- bias2: bfloat16 [512], replicated, may hold values from -3 to 3
Outputs:
- embedding: bfloat16 [32768, 512], P('vert')
The draws below stay inside these ranges and needn't reach their ends.
Inputs may be any that keep to these rules, and one draw needn't show every extreme that they name: `mirror_count`: some device has all 4 slots live on every peer, and some device receives 4 live rows from every device. `tile_count`: some device has all 128 tiles live.
All inputs are finite; a program needn't handle non-finite values. No bound on the sum of `tile_mask` on one device may be relied on, other than what follows from the above.
Results may differ from the reference program's by a relative error of at most 0.0051.
Values may be sent and summed in bfloat16 or wider, within the bound.
A program may use at most 128 MiB of HBM per device.

```python
import math
import jax
import jax.numpy as jnp
import numpy as np
from jax import lax

F = 512
TB = 128
NODE_DEV = 1024
MR = 4
TILES_DEV = 128
NODES = 32768
TBLK = 9
N_VERT = 32


def draw_mirror_count(key, part):
    first, second, third = jax.random.split(key, 3)
    base = jax.random.randint(first, (N_VERT, N_VERT), 1, MR + 1, dtype=jnp.int32)
    ranked = jax.random.permutation(second, N_VERT)
    hubs = ranked < max(N_VERT // 8, 1)
    column = jax.random.randint(third, (), 0, N_VERT, dtype=jnp.int32)
    filled = jnp.where(hubs[:, None], MR, base)
    return jnp.where(jnp.arange(N_VERT, dtype=jnp.int32)[None, :] == column, MR, filled).astype(jnp.int32)


def draw_tile_count(key, part):
    first, second = jax.random.split(key, 2)
    base = jax.random.randint(first, (N_VERT,), TILES_DEV // 4, TILES_DEV + 1, dtype=jnp.int32)
    busiest = jax.random.randint(second, (), 0, N_VERT, dtype=jnp.int32)
    return jnp.where(jnp.arange(N_VERT, dtype=jnp.int32) == busiest, TILES_DEV, base).astype(jnp.int32)


def place_ends(entries, own_key, least, top_value):
    index_at = [jax.random.randint(jax.random.fold_in(own_key, axis), (), 0, length) for axis, length in enumerate(entries.shape)]
    longest = entries.shape.index(max(entries.shape))
    next_to = index_at[:longest] + [(index_at[longest] + 1) % entries.shape[longest]] + index_at[longest + 1:]
    return entries.at[tuple(index_at)].set(least).at[tuple(next_to)].set(top_value)


def block_levels(key, dims, pieces, least, largest):
    factor_of = 1.0
    for axis_at, blocks in pieces:
        draws = jax.random.uniform(jax.random.fold_in(jax.random.fold_in(key, 6), axis_at), (blocks,), jnp.float32, least / len(pieces), largest / len(pieces))
        factor_of = factor_of * jnp.repeat(jnp.exp(draws), dims[axis_at] // blocks).reshape((-1,) + (1,) * (len(dims) - 1 - axis_at))
    return factor_of


def rank_bounds(amount, skew):
    loads = [(1 << 20) // math.isqrt(grade ** skew) + 1 for grade in range(1, amount + 1)]
    scale = 1 + sum(loads) // (1 << 30)
    return np.cumsum(np.array([max(1, weight // scale) for weight in loads]))


def skewed_ids(own_key, dims, amount, lean):
    grid = rank_bounds(amount, lean)
    pick = jax.random.randint(jax.random.fold_in(own_key, 1), dims, 0, int(grid[amount - 1]))
    grade = jnp.searchsorted(jnp.asarray(grid, jnp.int32), pick, side="right")
    return jax.random.permutation(jax.random.fold_in(own_key, 2), amount)[grade].astype(jnp.int32)


def bell_draw(own_key, extent, deviation, bound, pieces=(), kind=jnp.bfloat16):
    entries = deviation * jax.random.normal(own_key, extent, jnp.float32)
    if pieces:
        entries = entries * block_levels(own_key, extent, pieces, -0.22, 0.18)
    return jnp.clip(entries, -bound, bound).astype(kind)


def setup_inputs(seed: int = 0) -> dict:
    splits = jax.random.split(jax.random.key(seed), 13)
    features = bell_draw(splits[0], (NODES, F), 1.0, 6.0, ((0, 32),))
    send_rows = place_ends(skewed_ids(splits[1], (N_VERT, N_VERT, MR), NODE_DEV, 2), jax.random.fold_in(splits[1], 3), 0, NODE_DEV - 1).astype(jnp.int32)
    mirror_count = draw_mirror_count(jax.random.fold_in(splits[12], 71), 0)
    tile_coord = place_ends(jax.random.randint(splits[3], (N_VERT, 2, TILES_DEV), 0, TBLK), jax.random.fold_in(splits[3], 1), 0, TBLK - 1).astype(jnp.int32)
    tile_mask = place_ends((jax.random.randint(splits[4], (N_VERT, TILES_DEV, TB, TB), 0, 8) < 1).astype(jnp.int32), jax.random.fold_in(splits[4], 1), 0, 1)
    tile_count = draw_tile_count(jax.random.fold_in(splits[12], 71), 0)
    w_self1 = bell_draw(splits[6], (F, F), F ** -0.5, 0.25)
    w_neigh1 = bell_draw(splits[7], (F, F), (F // 16) ** -0.5, 1.0)
    bias1 = bell_draw(splits[8], (F,), 0.5, 3.0)
    w_self2 = bell_draw(splits[9], (F, F), F ** -0.5, 0.25)
    w_neigh2 = bell_draw(splits[10], (F, F), (F // 16) ** -0.5, 1.0)
    bias2 = bell_draw(splits[11], (F,), 0.5, 3.0)
    return dict(features=features, send_rows=send_rows, mirror_count=mirror_count, tile_coord=tile_coord, tile_mask=tile_mask, tile_count=tile_count, w_self1=w_self1, w_neigh1=w_neigh1, bias1=bias1, w_self2=w_self2, w_neigh2=w_neigh2, bias2=bias2)


def reference(features, send_rows, mirror_count, tile_coord, tile_mask, tile_count, w_self1, w_neigh1, bias1, w_self2, w_neigh2, bias2):
    nodes, width = features.shape
    number = send_rows.shape[0]
    own_rows = nodes // number
    slots = send_rows.shape[2]
    block = tile_mask.shape[2]
    tiles = tile_mask.shape[1]
    peers = jnp.arange(number, dtype=jnp.int32)

    def layout(device):
        mirror_ids = peers[:, None] * own_rows + send_rows[:, device, :].astype(jnp.int32)
        mirror_live = jnp.arange(slots, dtype=jnp.int32)[None, :] < mirror_count[:, device][:, None]
        ids = jnp.concatenate([device * own_rows + jnp.arange(own_rows, dtype=jnp.int32), mirror_ids.reshape(-1)])
        alive = jnp.concatenate([jnp.ones((own_rows,), bool), mirror_live.reshape(-1)])
        return ids.astype(jnp.int32), alive

    def aggregate(current):
        values = current.astype(jnp.float32)

        def visit(carry, device):
            totals, degree = carry
            ids, alive = layout(device)
            table = values[ids].reshape(-1, block, width)
            live_source = alive.astype(jnp.float32).reshape(-1, block)
            used = (jnp.arange(tiles, dtype=jnp.int32) < tile_count[device]).astype(jnp.float32)
            target = tile_coord[device, 0]
            source = tile_coord[device, 1]
            weights = tile_mask[device].astype(jnp.float32) * used[:, None, None] * live_source[source][:, None, :]
            products = jnp.einsum("tij,tjf->tif", weights, table[source], precision=lax.Precision.HIGHEST)
            local = jnp.zeros(table.shape, jnp.float32).at[target].add(products).reshape(-1, width)
            counted = jnp.zeros(live_source.shape, jnp.float32).at[target].add(jnp.sum(weights, axis=2)).reshape(-1)
            keep = alive.astype(jnp.float32)
            totals = totals.at[ids].add(local * keep[:, None])
            degree = degree.at[ids].add(counted * keep)
            return (totals, degree), None

        start = (jnp.zeros((nodes, width), jnp.float32), jnp.zeros((nodes,), jnp.float32))
        (totals, degree), _ = lax.scan(visit, start, peers)
        return totals, degree

    current = features
    for layer, (w_self, w_neigh, bias) in enumerate(((w_self1, w_neigh1, bias1), (w_self2, w_neigh2, bias2))):
        summed, degree = aggregate(current)
        mean = ((summed + current.astype(jnp.float32)) / (degree + 1.0)[:, None]).astype(jnp.bfloat16)
        pre = jnp.dot(current, w_self, preferred_element_type=jnp.float32) + jnp.dot(mean, w_neigh, preferred_element_type=jnp.float32) + bias.astype(jnp.float32)
        if layer == 0:
            current = jax.nn.relu(pre).astype(jnp.bfloat16)
        else:
            current = pre.astype(jnp.bfloat16)
    return current
```

```python
import functools

import jax
import jax.numpy as jnp
from jax import lax
from jax.experimental import pallas as pl
from jax.experimental.pallas import tpu as pltpu
from jax.sharding import PartitionSpec as P

LANES = 128
DEAD = 64.0
BF = jnp.bfloat16
F32 = jnp.float32


def mm(a, b):
    return jnp.dot(a, b, preferred_element_type=F32)


def count_kernel(group, coord, count, mask, out, held, sems):
    tiles, block, _ = mask.shape
    size = out.shape[0]
    live = count[0]
    groups = tiles // group

    def copy(g):
        span = pl.ds(g * group, group)
        return pltpu.make_async_copy(mask.at[span], held.at[span], sems.at[g])

    for g in range(groups):

        @pl.when(g * group < live)
        def _():
            copy(g).start()

    step = block

    @pl.loop(0, size // step)
    def _(b):
        rows = lax.broadcasted_iota(jnp.int32, (step, size), 0) + b * step
        cols = lax.broadcasted_iota(jnp.int32, (step, size), 1)
        out[pl.ds(pl.multiple_of(b * step, step), step), :] = jnp.where(rows == cols, 1.0, 0.0).astype(BF)

    for g in range(groups):

        @pl.when(g * group < live)
        def _():
            copy(g).wait()

            @pl.loop(g * group, jnp.minimum((g + 1) * group, live))
            def _(t):
                rows = pl.ds(pl.multiple_of(coord[0, t] * block, block), block)
                cols = pl.ds(pl.multiple_of(coord[1, t] * block, block), block)
                out[rows, cols] += held[t].astype(F32).astype(BF)


def count_edges(coord, count, mask, size):
    tiles, block, _ = mask.shape
    group = 8
    return pl.pallas_call(
        functools.partial(count_kernel, group),
        out_shape=jax.ShapeDtypeStruct((size, size), BF),
        in_specs=[
            pl.BlockSpec(memory_space=pltpu.SMEM),
            pl.BlockSpec(memory_space=pltpu.SMEM),
            pl.BlockSpec(memory_space=pl.ANY),
        ],
        out_specs=pl.BlockSpec(memory_space=pltpu.VMEM),
        scratch_shapes=[
            pltpu.VMEM(mask.shape, jnp.int32),
            pltpu.SemaphoreType.DMA((tiles // group,)),
        ],
        name="count_edges",
    )(coord, count, mask)


def layers_kernel(
    number,
    slots,
    step,
    feat_hbm,
    a_hbm,
    enc_col,
    enc_row,
    ws1_hbm,
    wn1_hbm,
    b1,
    ws2_hbm,
    wn2_hbm,
    b2,
    out_hbm,
    table,
    a,
    ws1,
    wn1,
    ws2,
    wn2,
    pick,
    spread,
    acc,
    selfp,
    denom,
    live_m,
    outv,
    sent,
    came,
    sent_n,
    came_n,
    load_sem,
    out_sem,
    send_sem,
    recv_sem,
    own_sem,
    n_sem,
):
    me = lax.axis_index("vert")
    rows, width = feat_hbm.shape
    mir = number * slots
    kb = width // LANES
    chunk = slots * kb
    flat = mir * kb
    size = rows + mir

    barrier = pltpu.get_barrier_semaphore()

    @pl.loop(1, number)
    def _(s):
        pl.semaphore_signal(barrier, inc=1, device_id=(lax.rem(me + s, number),), device_id_type=pl.DeviceIdType.MESH)

    loads = [
        pltpu.make_async_copy(feat_hbm, table.at[pl.ds(0, rows)], load_sem.at[0]),
        pltpu.make_async_copy(a_hbm, a, load_sem.at[1]),
        pltpu.make_async_copy(ws1_hbm, ws1, load_sem.at[2]),
        pltpu.make_async_copy(wn1_hbm, wn1, load_sem.at[3]),
        pltpu.make_async_copy(ws2_hbm, ws2, load_sem.at[4]),
        pltpu.make_async_copy(wn2_hbm, wn2, load_sem.at[5]),
    ]
    for load in loads:
        load.start()

    def iota(shape, dim):
        return lax.broadcasted_iota(jnp.int32, shape, dim)

    def one_hot(cond):
        return jnp.where(cond, 1.0, 0.0).astype(BF)

    pick[...] = one_hot(iota((mir, rows), 1) == enc_col[...])
    live_s = enc_col[...] >= 0
    spread[...] = one_hot(iota((rows, mir), 0) == enc_row[...])
    fr = iota((flat, mir), 0)
    to_flat = one_hot((fr // chunk) * slots + fr % slots == iota((flat, mir), 1))
    fc = iota((mir, flat), 1)
    from_flat = one_hot((fc // chunk) * slots + fc % slots == iota((mir, flat), 0))
    part = (iota((flat, LANES), 0) % chunk) // slots

    def pack(phase, value):
        wide = mm(to_flat, value)
        total = jnp.zeros((flat, LANES), F32)
        for k in range(kb):
            total = jnp.where(part == k, wide[:, k * LANES : (k + 1) * LANES], total)
        sent[phase] = total.astype(BF)

    def unpack(phase):
        narrow = came[phase]
        zero = jnp.zeros_like(narrow)
        wide = jnp.concatenate([jnp.where(part == k, narrow, zero) for k in range(kb)], axis=1)
        return mm(from_flat, wide)

    def send(phase):
        pltpu.make_async_copy(
            sent.at[phase, pl.ds(me * chunk, chunk)], came.at[phase, pl.ds(me * chunk, chunk)], own_sem.at[phase]
        ).start()

        @pl.loop(1, number)
        def _(s):
            dst = lax.rem(me + s, number)
            pltpu.make_async_remote_copy(
                src_ref=sent.at[phase, pl.ds(dst * chunk, chunk)],
                dst_ref=came.at[phase, pl.ds(me * chunk, chunk)],
                send_sem=send_sem.at[phase],
                recv_sem=recv_sem.at[phase],
                device_id=(dst,),
                device_id_type=pl.DeviceIdType.MESH,
            ).start()

    def wait_bytes(ref, sem):
        pltpu.make_async_copy(ref, ref, sem).wait()

    others = pl.ds(0, (number - 1) * chunk)

    def arrive(phase):
        pltpu.make_async_copy(
            sent.at[phase, pl.ds(me * chunk, chunk)], came.at[phase, pl.ds(me * chunk, chunk)], own_sem.at[phase]
        ).wait()
        wait_bytes(came.at[phase, others], recv_sem.at[phase])

    blocks = rows // step

    def over_rows(fn):
        @pl.loop(0, blocks)
        def _(b):
            fn(pl.ds(pl.multiple_of(b * step, step), step))

    loads[0].wait()
    gathered = mm(pick[...], table[pl.ds(0, rows), :])
    feat_s = gathered.astype(BF)
    pack(0, jnp.where(live_s, gathered, DEAD).astype(BF))
    pl.semaphore_wait(barrier, number - 1)
    send(0)

    loads[2].wait()

    def self1(span):
        selfp[span, :] = mm(table[span, :], ws1[...]) + b1[...].astype(F32)

    over_rows(self1)
    self_s = mm(feat_s, ws1[...]) + b1[...].astype(F32)
    same = mm(pick[...], spread[...]).astype(BF)
    loads[1].wait()
    a_s = mm(pick[...], a[pl.ds(0, rows), :]).astype(BF)

    arrive(0)
    got = unpack(0)
    alive = got[:, :1] < DEAD / 2
    live_m[...] = jnp.broadcast_to(one_hot(alive), (mir, LANES))
    table[pl.ds(rows, mir), :] = jnp.where(alive, got, 0.0).astype(BF)
    ones = jnp.concatenate([jnp.ones((rows, LANES), BF), live_m[...]], axis=0)

    a_m = a[pl.ds(rows, mir), :]
    diag = one_hot(iota((mir, size), 1) == iota((mir, size), 0) + rows)
    a_m = a_m - diag
    a[pl.ds(rows, mir), :] = a_m
    pack(1, mm(a_m, table[...]).astype(BF))
    send(1)
    counted = mm(a_m, ones)[:, :1]
    high = jnp.floor(counted * (1.0 / 256.0))
    low = counted - high * 256.0
    slot_of = iota((mir, mir), 0) % slots
    at_me = iota((mir, mir), 1) == me * slots + slot_of
    by_peer = one_hot(iota((number, mir), 1) // slots == iota((number, mir), 0))
    sent_n[:, 0, :] = mm(by_peer, jnp.where(at_me, high, 0.0).astype(BF)) * 256.0 + mm(
        by_peer, jnp.where(at_me, low, 0.0).astype(BF)
    )
    own_n = pltpu.make_async_copy(sent_n.at[me], came_n.at[me], n_sem.at[0])
    own_n.start()

    @pl.loop(1, number)
    def _(s):
        dst = lax.rem(me + s, number)
        pltpu.make_async_remote_copy(
            src_ref=sent_n.at[dst],
            dst_ref=came_n.at[me],
            send_sem=n_sem.at[1],
            recv_sem=n_sem.at[2],
            device_id=(dst,),
            device_id_type=pl.DeviceIdType.MESH,
        ).start()

    acc_s = mm(a_s, table[...])
    denom_s = mm(a_s, ones)[:, :1]

    def own1(span):
        acc[span, :] = mm(a[span, :], table[...])
        denom[span, :] = mm(a[span, :], ones)

    over_rows(own1)
    loads[3].wait()

    own_n.wait()
    wait_bytes(came_n.at[pl.ds(0, number - 1)], n_sem.at[2])
    counts = jnp.sum(came_n[:, 0, :], axis=0, keepdims=True)
    denom_s = denom_s + jnp.sum(same.astype(F32) * counts, axis=1, keepdims=True)

    arrive(1)
    ret = unpack(1).astype(BF)
    mean_s = ((acc_s + mm(same, ret)) / jnp.maximum(denom_s, 1.0)).astype(BF)
    hid_s = jnp.maximum(self_s + mm(mean_s, wn1[...]), 0.0).astype(BF)
    pack(2, hid_s)
    send(2)

    def hidden(span):
        full = denom[span, :1] + jnp.sum(spread[span, :].astype(F32) * counts, axis=1, keepdims=True)
        denom[span, :] = jnp.broadcast_to(full, (step, LANES))
        mean = ((acc[span, :] + mm(spread[span, :], ret)) / full).astype(BF)
        table[span, :] = jnp.maximum(selfp[span, :] + mm(mean, wn1[...]), 0.0).astype(BF)

    over_rows(hidden)
    partial = mm(a[pl.ds(rows, mir), pl.ds(0, rows)], table[pl.ds(0, rows), :])
    loads[4].wait()

    def self2(span):
        selfp[span, :] = mm(table[span, :], ws2[...]) + b2[...].astype(F32)

    over_rows(self2)

    def own2(span):
        acc[span, :] = mm(a[span, pl.ds(0, rows)], table[pl.ds(0, rows), :])

    over_rows(own2)
    loads[5].wait()

    arrive(2)
    second = (unpack(2) * live_m[:, :1].astype(F32)).astype(BF)
    table[pl.ds(rows, mir), :] = second
    pack(3, (partial + mm(a[pl.ds(rows, mir), pl.ds(rows, mir)], second)).astype(BF))
    send(3)

    def more2(span):
        acc[span, :] += mm(a[span, pl.ds(rows, mir)], table[pl.ds(rows, mir), :])

    over_rows(more2)
    arrive(3)
    ret2 = unpack(3).astype(BF)

    def last(span):
        mean = ((acc[span, :] + mm(spread[span, :], ret2)) / denom[span, :1]).astype(BF)
        outv[span, :] = (selfp[span, :] + mm(mean, wn2[...])).astype(BF)

    over_rows(last)
    flush = pltpu.make_async_copy(outv, out_hbm, out_sem)
    flush.start()
    for phase in range(4):
        wait_bytes(sent.at[phase, others], send_sem.at[phase])
    wait_bytes(sent_n.at[pl.ds(0, number - 1)], n_sem.at[1])
    flush.wait()


def run_layers(number, slots, features, a, enc, w_self1, w_neigh1, bias1, w_self2, w_neigh2, bias2):
    rows, width = features.shape
    mir = number * slots
    size = rows + mir
    flat = mir * (width // LANES)
    any_spec = pl.BlockSpec(memory_space=pl.ANY)
    vm = pl.BlockSpec(memory_space=pltpu.VMEM)
    step = 256
    return pl.pallas_call(
        functools.partial(layers_kernel, number, slots, step),
        out_shape=jax.ShapeDtypeStruct((rows, width), BF),
        in_specs=[any_spec, any_spec, vm, vm, any_spec, any_spec, vm, any_spec, any_spec, vm],
        out_specs=any_spec,
        scratch_shapes=[
            pltpu.VMEM((size, width), BF),
            pltpu.VMEM((size, size), BF),
            pltpu.VMEM((width, width), BF),
            pltpu.VMEM((width, width), BF),
            pltpu.VMEM((width, width), BF),
            pltpu.VMEM((width, width), BF),
            pltpu.VMEM((mir, rows), BF),
            pltpu.VMEM((rows, mir), BF),
            pltpu.VMEM((rows, width), F32),
            pltpu.VMEM((rows, width), F32),
            pltpu.VMEM((rows, LANES), F32),
            pltpu.VMEM((mir, LANES), BF),
            pltpu.VMEM((rows, width), BF),
            pltpu.VMEM((4, flat, LANES), BF),
            pltpu.VMEM((4, flat, LANES), BF),
            pltpu.VMEM((number, 1, mir), F32),
            pltpu.VMEM((number, 1, mir), F32),
            pltpu.SemaphoreType.DMA((6,)),
            pltpu.SemaphoreType.DMA,
            pltpu.SemaphoreType.DMA((4,)),
            pltpu.SemaphoreType.DMA((4,)),
            pltpu.SemaphoreType.DMA((4,)),
            pltpu.SemaphoreType.DMA((3,)),
        ],
        compiler_params=pltpu.CompilerParams(
            collective_id=0, has_side_effects=True, vmem_limit_bytes=60 * 1024 * 1024
        ),
        name="layers",
    )(
        features,
        a,
        enc.reshape(mir, 1),
        enc.reshape(1, mir),
        w_self1,
        w_neigh1,
        bias1.reshape(1, width),
        w_self2,
        w_neigh2,
        bias2.reshape(1, width),
    )


def body(
    features,
    send_rows,
    mirror_count,
    tile_coord,
    tile_mask,
    tile_count,
    w_self1,
    w_neigh1,
    bias1,
    w_self2,
    w_neigh2,
    bias2,
):
    number = lax.axis_size("vert")
    rows, _ = features.shape
    slots = send_rows.shape[2]
    live = jnp.arange(slots, dtype=jnp.int32)[None, :] < mirror_count[0][:, None]
    enc = jnp.where(live, send_rows[0], -1)
    a = count_edges(tile_coord[0], tile_count, tile_mask[0], rows + number * slots)
    return run_layers(number, slots, features, a, enc, w_self1, w_neigh1, bias1, w_self2, w_neigh2, bias2)


def solution(mesh):
    in_specs = (
        P("vert", None),
        P("vert", None, None),
        P("vert", None),
        P("vert", None, None),
        P("vert", None, None, None),
        P("vert"),
        P(),
        P(),
        P(),
        P(),
        P(),
        P(),
    )
    out_specs = P("vert", None)
    return jax.shard_map(body, mesh=mesh, in_specs=in_specs, out_specs=out_specs, check_vma=False)
```

```python
import functools

import jax
import jax.numpy as jnp
from jax import lax
from jax.experimental import pallas as pl
from jax.experimental.pallas import tpu as pltpu
from jax.sharding import PartitionSpec as P

LANES = 128
DEAD = 64.0
BF = jnp.bfloat16
F32 = jnp.float32


def mm(a, b):
    return jnp.dot(a, b, preferred_element_type=F32)


def layers_kernel(
    number,
    slots,
    step,
    feat_hbm,
    send_rows,
    mirror_count,
    coord,
    mask_hbm,
    tile_count,
    ws1_hbm,
    wn1_hbm,
    b1,
    ws2_hbm,
    wn2_hbm,
    b2,
    out_hbm,
    table,
    a,
    held,
    prefix,
    links,
    link_s,
    ws1,
    wn1,
    ws2,
    wn2,
    pick,
    spread,
    acc,
    selfp,
    denom,
    live_m,
    outv,
    sent,
    came,
    sent_n,
    came_n,
    load_sem,
    mask_sem,
    link_sem,
    out_sem,
    send_sem,
    recv_sem,
    own_sem,
    n_sem,
):
    me = lax.axis_index("vert")
    rows, width = feat_hbm.shape
    mir = number * slots
    kb = width // LANES
    chunk = slots * kb
    flat = mir * kb
    size = rows + mir

    barrier = pltpu.get_barrier_semaphore()

    @pl.loop(1, number)
    def _(s):
        pl.semaphore_signal(barrier, inc=1, device_id=(lax.rem(me + s, number),), device_id_type=pl.DeviceIdType.MESH)

    loads = [
        pltpu.make_async_copy(feat_hbm, table.at[pl.ds(0, rows)], load_sem.at[0]),
        pltpu.make_async_copy(ws1_hbm, ws1, load_sem.at[1]),
        pltpu.make_async_copy(wn1_hbm, wn1, load_sem.at[2]),
        pltpu.make_async_copy(ws2_hbm, ws2, load_sem.at[3]),
        pltpu.make_async_copy(wn2_hbm, wn2, load_sem.at[4]),
    ]
    tiles, block = mask_hbm.shape[1], mask_hbm.shape[2]
    groups = mask_sem.shape[0]
    group = tiles // groups
    blocks_a = size // block

    def mask_copy(g):
        span = pl.ds(g * group, group)
        return pltpu.make_async_copy(mask_hbm.at[0, span], held.at[span], mask_sem.at[g])

    loads[0].start()
    for g in range(groups):
        mask_copy(g).start()
    for load in loads[1:]:
        load.start()

    def iota(shape, dim):
        return lax.broadcasted_iota(jnp.int32, shape, dim)

    def one_hot(cond):
        return jnp.where(cond, 1.0, 0.0).astype(BF)

    def column_to_row(col, height):
        return jnp.transpose(jnp.broadcast_to(col, (col.shape[0], height)))[:1, :]

    key_row = (coord[0, :1, :] * blocks_a + coord[0, 1:2, :]).astype(F32)
    key_col = jnp.transpose(jnp.broadcast_to(key_row, (LANES, tiles)))[:, :1].astype(jnp.int32)
    key_row = key_row.astype(jnp.int32)
    place = iota((tiles, tiles), 0)
    before = jnp.where((key_col == key_row) & (place < iota((tiles, tiles), 1)), place + 1, 0)
    wide_links = links.shape[1]
    links[...] = jnp.zeros_like(links)
    links[0:1, pl.ds(0, tiles)] = jnp.max(before, axis=0, keepdims=True)
    spot = iota((tiles, wide_links), 0)
    ended = (key_col == iota((tiles, wide_links), 1)) & (spot < tile_count[0])
    links[1:2, :] = jnp.max(jnp.where(ended, spot + 1, 0), axis=0, keepdims=True)
    to_scalar = pltpu.make_async_copy(links, link_s, link_sem)
    to_scalar.start()

    slot_col = iota((mir, 1), 0) % slots
    expand = one_hot(slot_col == iota((mir, slots), 1))
    raw = send_rows[0]
    each = mm(expand, (raw // 256).astype(F32).astype(BF)) * 256.0 + mm(expand, (raw % 256).astype(F32).astype(BF))
    peer_hit = iota((mir, number), 1) == iota((mir, number), 0) // slots
    row_col = jnp.sum(jnp.where(peer_hit, each, 0.0), axis=1, keepdims=True)
    count_col = jnp.sum(jnp.where(peer_hit, mirror_count[...], 0).astype(F32), axis=1, keepdims=True)
    enc_f = jnp.where(slot_col.astype(F32) < count_col, row_col, -1.0)
    enc_col = enc_f.astype(jnp.int32)
    enc_row = column_to_row(enc_f, LANES).astype(jnp.int32)

    pick[...] = one_hot(iota((mir, rows), 1) == enc_col)
    live_s = enc_col >= 0
    spread[...] = one_hot(iota((rows, mir), 0) == enc_row)
    fr = iota((flat, mir), 0)
    to_flat = one_hot((fr // chunk) * slots + fr % slots == iota((flat, mir), 1))
    fc = iota((mir, flat), 1)
    from_flat = one_hot((fc // chunk) * slots + fc % slots == iota((mir, flat), 0))
    part = (iota((flat, LANES), 0) % chunk) // slots

    def pack(phase, value):
        wide = mm(to_flat, value)
        total = jnp.zeros((flat, LANES), F32)
        for k in range(kb):
            total = jnp.where(part == k, wide[:, k * LANES : (k + 1) * LANES], total)
        sent[phase] = total.astype(BF)

    def unpack(phase):
        narrow = came[phase]
        zero = jnp.zeros_like(narrow)
        wide = jnp.concatenate([jnp.where(part == k, narrow, zero) for k in range(kb)], axis=1)
        return mm(from_flat, wide)

    def send(phase):
        pltpu.make_async_copy(
            sent.at[phase, pl.ds(me * chunk, chunk)], came.at[phase, pl.ds(me * chunk, chunk)], own_sem.at[phase]
        ).start()

        @pl.loop(1, number)
        def _(s):
            dst = lax.rem(me + s, number)
            pltpu.make_async_remote_copy(
                src_ref=sent.at[phase, pl.ds(dst * chunk, chunk)],
                dst_ref=came.at[phase, pl.ds(me * chunk, chunk)],
                send_sem=send_sem.at[phase],
                recv_sem=recv_sem.at[phase],
                device_id=(dst,),
                device_id_type=pl.DeviceIdType.MESH,
            ).start()

    def wait_bytes(ref, sem):
        pltpu.make_async_copy(ref, ref, sem).wait()

    others = pl.ds(0, (number - 1) * chunk)

    def arrive(phase):
        pltpu.make_async_copy(
            sent.at[phase, pl.ds(me * chunk, chunk)], came.at[phase, pl.ds(me * chunk, chunk)], own_sem.at[phase]
        ).wait()
        wait_bytes(came.at[phase, others], recv_sem.at[phase])

    blocks = rows // step

    def over_rows(fn):
        @pl.loop(0, blocks)
        def _(b):
            fn(pl.ds(pl.multiple_of(b * step, step), step))

    loads[0].wait()
    gathered = mm(pick[...], table[pl.ds(0, rows), :])
    feat_s = gathered.astype(BF)
    pack(0, jnp.where(live_s, gathered, DEAD).astype(BF))
    pl.semaphore_wait(barrier, number - 1)
    send(0)

    to_scalar.wait()
    prefix[0] = jnp.zeros((block, block), BF)
    for g in range(groups):
        mask_copy(g).wait()

        @pl.loop(g * group, (g + 1) * group, unroll=4)
        def _(t):
            prefix[t + 1] = held[t].astype(F32).astype(BF) + prefix[link_s[0, t]]

    eye = one_hot(iota((block, block), 0) == iota((block, block), 1))
    for b in range(blocks_a):
        for c in range(blocks_a):
            piece = prefix[link_s[1, b * blocks_a + c]]
            if b == c and b < rows // block:
                piece = piece + eye
            a[b * block : (b + 1) * block, c * block : (c + 1) * block] = piece

    loads[1].wait()

    def self1(span):
        selfp[span, :] = mm(table[span, :], ws1[...]) + b1[...].astype(F32)[None, :]

    over_rows(self1)
    self_s = mm(feat_s, ws1[...]) + b1[...].astype(F32)[None, :]
    same = mm(pick[...], spread[...]).astype(BF)
    a_s = mm(pick[...], a[pl.ds(0, rows), :]).astype(BF)

    arrive(0)
    got = unpack(0)
    alive = got[:, :1] < DEAD / 2
    live_m[...] = jnp.broadcast_to(one_hot(alive), (mir, LANES))
    table[pl.ds(rows, mir), :] = jnp.where(alive, got, 0.0).astype(BF)
    ones = jnp.concatenate([jnp.ones((rows, LANES), BF), live_m[...]], axis=0)

    a_m = a[pl.ds(rows, mir), :]
    pack(1, mm(a_m, table[...]).astype(BF))
    send(1)
    counted = mm(a_m, ones)[:, :1]
    high = jnp.floor(counted * (1.0 / 256.0))
    low = counted - high * 256.0
    slot_of = iota((mir, mir), 0) % slots
    at_me = iota((mir, mir), 1) == me * slots + slot_of
    by_peer = one_hot(iota((number, mir), 1) // slots == iota((number, mir), 0))
    sent_n[:, 0, :] = mm(by_peer, jnp.where(at_me, high, 0.0).astype(BF)) * 256.0 + mm(
        by_peer, jnp.where(at_me, low, 0.0).astype(BF)
    )
    own_n = pltpu.make_async_copy(sent_n.at[me], came_n.at[me], n_sem.at[0])
    own_n.start()

    @pl.loop(1, number)
    def _(s):
        dst = lax.rem(me + s, number)
        pltpu.make_async_remote_copy(
            src_ref=sent_n.at[dst],
            dst_ref=came_n.at[me],
            send_sem=n_sem.at[1],
            recv_sem=n_sem.at[2],
            device_id=(dst,),
            device_id_type=pl.DeviceIdType.MESH,
        ).start()

    acc_s = mm(a_s, table[...])
    denom_s = mm(a_s, ones)[:, :1]

    def own1(span):
        acc[span, :] = mm(a[span, :], table[...])
        denom[span, :] = mm(a[span, :], ones)

    over_rows(own1)
    loads[2].wait()

    own_n.wait()
    wait_bytes(came_n.at[pl.ds(0, number - 1)], n_sem.at[2])
    counts = jnp.sum(came_n[:, 0, :], axis=0, keepdims=True)
    denom_s = denom_s + jnp.sum(same.astype(F32) * counts, axis=1, keepdims=True)

    arrive(1)
    ret = unpack(1).astype(BF)
    mean_s = ((acc_s + mm(same, ret)) / jnp.maximum(denom_s, 1.0)).astype(BF)
    hid_s = jnp.maximum(self_s + mm(mean_s, wn1[...]), 0.0).astype(BF)
    pack(2, hid_s)
    send(2)

    def hidden(span):
        full = denom[span, :1] + jnp.sum(spread[span, :].astype(F32) * counts, axis=1, keepdims=True)
        denom[span, :] = jnp.broadcast_to(full, (step, LANES))
        mean = ((acc[span, :] + mm(spread[span, :], ret)) / full).astype(BF)
        table[span, :] = jnp.maximum(selfp[span, :] + mm(mean, wn1[...]), 0.0).astype(BF)

    over_rows(hidden)
    partial = mm(a[pl.ds(rows, mir), pl.ds(0, rows)], table[pl.ds(0, rows), :])
    loads[3].wait()

    def self2(span):
        selfp[span, :] = mm(table[span, :], ws2[...]) + b2[...].astype(F32)[None, :]

    over_rows(self2)

    def own2(span):
        acc[span, :] = mm(a[span, pl.ds(0, rows)], table[pl.ds(0, rows), :])

    over_rows(own2)
    loads[4].wait()

    arrive(2)
    second = (unpack(2) * live_m[:, :1].astype(F32)).astype(BF)
    table[pl.ds(rows, mir), :] = second
    pack(3, (partial + mm(a[pl.ds(rows, mir), pl.ds(rows, mir)], second)).astype(BF))
    send(3)

    def more2(span):
        acc[span, :] += mm(a[span, pl.ds(rows, mir)], table[pl.ds(rows, mir), :])

    over_rows(more2)
    arrive(3)
    ret2 = unpack(3).astype(BF)

    def last(span):
        mean = ((acc[span, :] + mm(spread[span, :], ret2)) / denom[span, :1]).astype(BF)
        outv[span, :] = (selfp[span, :] + mm(mean, wn2[...])).astype(BF)

    over_rows(last)
    flush = pltpu.make_async_copy(outv, out_hbm, out_sem)
    flush.start()
    for phase in range(4):
        wait_bytes(sent.at[phase, others], send_sem.at[phase])
    wait_bytes(sent_n.at[pl.ds(0, number - 1)], n_sem.at[1])
    flush.wait()


def body(
    features,
    send_rows,
    mirror_count,
    tile_coord,
    tile_mask,
    tile_count,
    w_self1,
    w_neigh1,
    bias1,
    w_self2,
    w_neigh2,
    bias2,
):
    number = lax.axis_size("vert")
    rows, width = features.shape
    slots = send_rows.shape[2]
    _, tiles, block, _ = tile_mask.shape
    mir = number * slots
    size = rows + mir
    flat = mir * (width // LANES)
    pairs = (size // block) ** 2
    wide_links = -(-max(pairs, tiles) // LANES) * LANES
    any_spec = pl.BlockSpec(memory_space=pl.ANY)
    vm = pl.BlockSpec(memory_space=pltpu.VMEM)
    sm = pl.BlockSpec(memory_space=pltpu.SMEM)
    step = 256
    return pl.pallas_call(
        functools.partial(layers_kernel, number, slots, step),
        out_shape=jax.ShapeDtypeStruct((rows, width), BF),
        in_specs=[any_spec, vm, vm, vm, any_spec, sm, any_spec, any_spec, vm, any_spec, any_spec, vm],
        out_specs=any_spec,
        scratch_shapes=[
            pltpu.VMEM((size, width), BF),
            pltpu.VMEM((size, size), BF),
            pltpu.VMEM((tiles, block, block), jnp.int32),
            pltpu.VMEM((tiles + 1, block, block), BF),
            pltpu.VMEM((8, wide_links), jnp.int32),
            pltpu.SMEM((8, wide_links), jnp.int32),
            pltpu.VMEM((width, width), BF),
            pltpu.VMEM((width, width), BF),
            pltpu.VMEM((width, width), BF),
            pltpu.VMEM((width, width), BF),
            pltpu.VMEM((mir, rows), BF),
            pltpu.VMEM((rows, mir), BF),
            pltpu.VMEM((rows, width), F32),
            pltpu.VMEM((rows, width), F32),
            pltpu.VMEM((rows, LANES), F32),
            pltpu.VMEM((mir, LANES), BF),
            pltpu.VMEM((rows, width), BF),
            pltpu.VMEM((4, flat, LANES), BF),
            pltpu.VMEM((4, flat, LANES), BF),
            pltpu.VMEM((number, 1, mir), F32),
            pltpu.VMEM((number, 1, mir), F32),
            pltpu.SemaphoreType.DMA((5,)),
            pltpu.SemaphoreType.DMA((8,)),
            pltpu.SemaphoreType.DMA,
            pltpu.SemaphoreType.DMA,
            pltpu.SemaphoreType.DMA((4,)),
            pltpu.SemaphoreType.DMA((4,)),
            pltpu.SemaphoreType.DMA((4,)),
            pltpu.SemaphoreType.DMA((3,)),
        ],
        compiler_params=pltpu.CompilerParams(
            collective_id=0, has_side_effects=True, vmem_limit_bytes=60 * 1024 * 1024
        ),
        name="layers",
    )(
        features,
        jnp.swapaxes(send_rows, 1, 2),
        mirror_count,
        tile_coord,
        tile_mask,
        tile_count,
        w_self1,
        w_neigh1,
        bias1,
        w_self2,
        w_neigh2,
        bias2,
    )


def solution(mesh):
    in_specs = (
        P("vert", None),
        P("vert", None, None),
        P("vert", None),
        P("vert", None, None),
        P("vert", None, None, None),
        P("vert"),
        P(),
        P(),
        P(),
        P(),
        P(),
        P(),
    )
    out_specs = P("vert", None)
    return jax.shard_map(body, mesh=mesh, in_specs=in_specs, out_specs=out_specs, check_vma=False)
```

```python
import functools

import jax
import jax.numpy as jnp
from jax import lax
from jax.experimental import pallas as pl
from jax.experimental.pallas import tpu as pltpu
from jax.sharding import PartitionSpec as P

LANES = 128
DEAD = 64.0
BF = jnp.bfloat16
F32 = jnp.float32


def div(x, n):
    return x >> (n.bit_length() - 1) if n & (n - 1) == 0 else x // n


def mod(x, n):
    return x & (n - 1) if n & (n - 1) == 0 else x % n


def mm(a, b):
    return jnp.dot(a, b, preferred_element_type=F32)


def layers_kernel(
    number,
    slots,
    step,
    feat_hbm,
    send_rows,
    mirror_count,
    coord,
    mask_hbm,
    tile_count,
    ws1_hbm,
    wn1_hbm,
    b1,
    ws2_hbm,
    wn2_hbm,
    b2,
    out_hbm,
    table,
    a,
    held,
    prefix,
    links,
    link_s,
    ws1,
    wn1,
    ws2,
    wn2,
    a_flat,
    a_packed,
    base,
    pick,
    spread,
    acc,
    selfp,
    denom,
    live_m,
    outv,
    sent,
    came,
    sent_n,
    came_n,
    load_sem,
    mask_sem,
    link_sem,
    out_sem,
    send_sem,
    recv_sem,
    own_sem,
    n_sem,
):
    me = lax.axis_index("vert")
    rows, width = feat_hbm.shape
    mir = number * slots
    kb = width // LANES
    chunk = slots * kb
    flat = mir * kb
    size = rows + mir

    barrier = pltpu.get_barrier_semaphore()

    @pl.loop(1, number)
    def _(s):
        pl.semaphore_signal(barrier, inc=1, device_id=(lax.rem(me + s, number),), device_id_type=pl.DeviceIdType.MESH)

    loads = [
        pltpu.make_async_copy(feat_hbm, table.at[pl.ds(0, rows)], load_sem.at[0]),
        pltpu.make_async_copy(ws1_hbm, ws1, load_sem.at[1]),
        pltpu.make_async_copy(wn1_hbm, wn1, load_sem.at[2]),
        pltpu.make_async_copy(ws2_hbm, ws2, load_sem.at[3]),
        pltpu.make_async_copy(wn2_hbm, wn2, load_sem.at[4]),
    ]
    tiles, block = mask_hbm.shape[1], mask_hbm.shape[2]
    groups = mask_sem.shape[0]
    group = tiles // groups
    blocks_a = size // block

    def mask_copy(g):
        span = pl.ds(g * group, group)
        return pltpu.make_async_copy(mask_hbm.at[0, span], held.at[span], mask_sem.at[g])

    loads[0].start()
    for g in range(groups):
        mask_copy(g).start()
    for load in loads[1:]:
        load.start()

    def iota(shape, dim):
        return lax.broadcasted_iota(jnp.int32, shape, dim)

    def one_hot(cond):
        return jnp.where(cond, 1.0, 0.0).astype(BF)

    def column_to_row(col, height):
        return jnp.transpose(jnp.broadcast_to(col, (col.shape[0], height)))[:1, :]

    key_row = (coord[0, :1, :] * blocks_a + coord[0, 1:2, :]).astype(F32)
    key_col = jnp.transpose(jnp.broadcast_to(key_row, (LANES, tiles)))[:, :1].astype(jnp.int32)
    key_row = key_row.astype(jnp.int32)
    place = iota((tiles, tiles), 0)
    before = jnp.where((key_col == key_row) & (place < iota((tiles, tiles), 1)), place + 1, 0)
    wide_links = links.shape[1]
    links[...] = jnp.zeros_like(links)
    links[0:1, pl.ds(0, tiles)] = jnp.max(before, axis=0, keepdims=True)
    spot = iota((tiles, wide_links), 0)
    ended = (key_col == iota((tiles, wide_links), 1)) & (spot < tile_count[0])
    links[1:2, :] = jnp.max(jnp.where(ended, spot + 1, 0), axis=0, keepdims=True)
    to_scalar = pltpu.make_async_copy(links, link_s, link_sem)
    to_scalar.start()

    slot_col = mod(iota((mir, 1), 0), slots)
    expand = one_hot(slot_col == iota((mir, slots), 1))
    raw = send_rows[0]
    each = mm(expand, (div(raw, 256)).astype(F32).astype(BF)) * 256.0 + mm(expand, (mod(raw, 256)).astype(F32).astype(BF))
    peer_hit = iota((mir, number), 1) == div(iota((mir, number), 0), slots)
    row_col = jnp.sum(jnp.where(peer_hit, each, 0.0), axis=1, keepdims=True)
    count_col = jnp.sum(jnp.where(peer_hit, mirror_count[...], 0).astype(F32), axis=1, keepdims=True)
    enc_f = jnp.where(slot_col.astype(F32) < count_col, row_col, -1.0)
    enc_col = enc_f.astype(jnp.int32)
    enc_row = column_to_row(enc_f, LANES).astype(jnp.int32)

    pick[...] = one_hot(iota((mir, rows), 1) == enc_col)
    live_s = enc_col >= 0
    spread[...] = one_hot(iota((rows, mir), 0) == enc_row)
    fr = iota((flat, mir), 0)
    to_flat = one_hot(div(fr, chunk) * slots + mod(fr, slots) == iota((flat, mir), 1))
    fc = iota((mir, flat), 1)
    from_flat = one_hot(div(fc, chunk) * slots + mod(fc, slots) == iota((mir, flat), 0))
    part = div(mod(iota((flat, LANES), 0), chunk), slots)

    def own_lanes(wide):
        total = wide[:, :LANES]
        for k in range(1, kb):
            total = jnp.where(part == k, wide[:, k * LANES : (k + 1) * LANES], total)
        return total

    def pack(phase, value):
        sent[phase] = own_lanes(mm(to_flat, value)).astype(BF)

    def widen(phase):
        narrow = came[phase]
        zero = jnp.zeros_like(narrow)
        return jnp.concatenate([jnp.where(part == k, narrow, zero) for k in range(kb)], axis=1)

    def unpack(phase):
        return mm(from_flat, widen(phase))

    def send(phase):
        pltpu.make_async_copy(
            sent.at[phase, pl.ds(me * chunk, chunk)], came.at[phase, pl.ds(me * chunk, chunk)], own_sem.at[phase]
        ).start()

        @pl.loop(1, number)
        def _(s):
            dst = lax.rem(me + s, number)
            pltpu.make_async_remote_copy(
                src_ref=sent.at[phase, pl.ds(dst * chunk, chunk)],
                dst_ref=came.at[phase, pl.ds(me * chunk, chunk)],
                send_sem=send_sem.at[phase],
                recv_sem=recv_sem.at[phase],
                device_id=(dst,),
                device_id_type=pl.DeviceIdType.MESH,
            ).start()

    def wait_bytes(ref, sem):
        pltpu.make_async_copy(ref, ref, sem).wait()

    others = pl.ds(0, (number - 1) * chunk)

    def arrive(phase):
        pltpu.make_async_copy(
            sent.at[phase, pl.ds(me * chunk, chunk)], came.at[phase, pl.ds(me * chunk, chunk)], own_sem.at[phase]
        ).wait()
        wait_bytes(came.at[phase, others], recv_sem.at[phase])

    blocks = rows // step

    def over_rows(fn):
        @pl.loop(0, blocks)
        def _(b):
            fn(pl.ds(pl.multiple_of(b * step, step), step))

    loads[0].wait()
    gathered = mm(pick[...], table[pl.ds(0, rows), :])
    feat_s = gathered.astype(BF)
    pack(0, jnp.where(live_s, gathered, DEAD).astype(BF))
    pl.semaphore_wait(barrier, number - 1)
    send(0)

    to_scalar.wait()
    prefix[0] = jnp.zeros((block, block), BF)
    for g in range(groups):
        mask_copy(g).wait()

        @pl.loop(g * group, (g + 1) * group, unroll=4)
        def _(t):
            prefix[t + 1] = held[t].astype(F32).astype(BF) + prefix[link_s[0, t]]

    eye = one_hot(iota((block, block), 0) == iota((block, block), 1))
    for b in range(blocks_a):
        for c in range(blocks_a):
            piece = prefix[link_s[1, b * blocks_a + c]]
            if b == c and b < rows // block:
                piece = piece + eye
            a[b * block : (b + 1) * block, c * block : (c + 1) * block] = piece

    a_flat[...] = mm(to_flat, a[pl.ds(rows, mir), pl.ds(0, rows)]).astype(BF)
    base[...] = own_lanes(mm(a_flat[...], table[pl.ds(0, rows), :]))
    a_rep = mm(to_flat, a[pl.ds(rows, mir), pl.ds(rows, mir)]).astype(BF)
    high = flat // 4
    for h in range(4):
        kr = div(mod(iota((high, flat), 0) + h * high, chunk), slots)
        kc = div(mod(iota((high, flat), 1), chunk), slots)
        piece = mm(a_rep[h * high : (h + 1) * high], from_flat)
        a_packed[h * high : (h + 1) * high, :] = jnp.where(kr == kc, piece, 0.0).astype(BF)

    arrive(0)
    fresh = came[0].astype(F32)
    clean = jnp.where(fresh < DEAD / 2, fresh, 0.0).astype(BF)
    sent[1] = (base[...] + mm(a_packed[...], clean)).astype(BF)
    send(1)

    got = unpack(0)
    alive = got[:, :1] < DEAD / 2
    live_m[...] = jnp.broadcast_to(one_hot(alive), (mir, LANES))
    table[pl.ds(rows, mir), :] = jnp.where(alive, got, 0.0).astype(BF)
    ones = jnp.concatenate([jnp.ones((rows, LANES), BF), live_m[...]], axis=0)
    a_m = a[pl.ds(rows, mir), :]
    counted = mm(a_m, ones)[:, :1]
    upper = jnp.floor(counted * (1.0 / 256.0))
    lower = counted - upper * 256.0
    slot_of = mod(iota((mir, mir), 0), slots)
    at_me = iota((mir, mir), 1) == me * slots + slot_of
    by_peer = one_hot(div(iota((number, mir), 1), slots) == iota((number, mir), 0))
    sent_n[:, 0, :] = mm(by_peer, jnp.where(at_me, upper, 0.0).astype(BF)) * 256.0 + mm(
        by_peer, jnp.where(at_me, lower, 0.0).astype(BF)
    )
    own_n = pltpu.make_async_copy(sent_n.at[me], came_n.at[me], n_sem.at[0])
    own_n.start()

    @pl.loop(1, number)
    def _(s):
        dst = lax.rem(me + s, number)
        pltpu.make_async_remote_copy(
            src_ref=sent_n.at[dst],
            dst_ref=came_n.at[me],
            send_sem=n_sem.at[1],
            recv_sem=n_sem.at[2],
            device_id=(dst,),
            device_id_type=pl.DeviceIdType.MESH,
        ).start()

    loads[1].wait()
    self_s = mm(feat_s, ws1[...]) + b1[...].astype(F32)[None, :]
    same = mm(pick[...], spread[...]).astype(BF)
    same_flat = mm(same, from_flat).astype(BF)
    a_s = mm(pick[...], a[pl.ds(0, rows), :]).astype(BF)
    acc_s = mm(a_s, table[...])
    denom_s = mm(a_s, ones)[:, :1]

    def own1(span):
        selfp[span, :] = mm(table[span, :], ws1[...]) + b1[...].astype(F32)[None, :]
        acc[span, :] = mm(a[span, :], table[...])
        denom[span, :] = mm(a[span, :], ones)

    over_rows(own1)
    loads[2].wait()

    own_n.wait()
    wait_bytes(came_n.at[pl.ds(0, number - 1)], n_sem.at[2])
    counts = jnp.sum(came_n[:, 0, :], axis=0, keepdims=True)
    denom_s = denom_s + jnp.sum(same.astype(F32) * counts, axis=1, keepdims=True)

    arrive(1)
    safe_s = jnp.maximum(denom_s, 1.0)
    mean_s = ((acc_s + mm(same_flat, widen(1))) / safe_s).astype(BF)
    hid_s = jnp.maximum(self_s + mm(mean_s, wn1[...]), 0.0)
    pack(2, jnp.where(live_s, hid_s, 0.0).astype(BF))
    send(2)
    ret = unpack(1).astype(BF)

    def hidden(span):
        full = denom[span, :1] + jnp.sum(spread[span, :].astype(F32) * counts, axis=1, keepdims=True)
        denom[span, :] = jnp.broadcast_to(full, (step, LANES))
        mean = ((acc[span, :] + mm(spread[span, :], ret)) / full).astype(BF)
        table[span, :] = jnp.maximum(selfp[span, :] + mm(mean, wn1[...]), 0.0).astype(BF)

    over_rows(hidden)
    base[...] = own_lanes(mm(a_flat[...], table[pl.ds(0, rows), :]))
    loads[3].wait()

    def self2(span):
        selfp[span, :] = mm(table[span, :], ws2[...]) + b2[...].astype(F32)[None, :]

    over_rows(self2)

    def own2(span):
        acc[span, :] = mm(a[span, pl.ds(0, rows)], table[pl.ds(0, rows), :])

    over_rows(own2)
    loads[4].wait()

    arrive(2)
    sent[3] = (base[...] + mm(a_packed[...], came[2])).astype(BF)
    send(3)
    table[pl.ds(rows, mir), :] = unpack(2).astype(BF)

    def early(span):
        total = acc[span, :] + mm(a[span, pl.ds(rows, mir)], table[pl.ds(rows, mir), :])
        mean = (total / denom[span, :1]).astype(BF)
        outv[span, :] = (selfp[span, :] + mm(mean, wn2[...])).astype(BF)

    over_rows(early)
    acc_s2 = mm(a_s, table[...])
    self_s2 = mm(hid_s.astype(BF), ws2[...]) + b2[...].astype(F32)[None, :]
    earlier = iota((mir, mir), 0) < iota((mir, mir), 1)
    again = jnp.max(jnp.where(earlier, same.astype(F32), 0.0), axis=0, keepdims=True)

    def firsts(span):
        spread[span, :] = jnp.where(again > 0.0, 0.0, spread[span, :].astype(F32)).astype(BF)

    over_rows(firsts)
    arrive(3)
    mean_s2 = ((acc_s2 + mm(same_flat, widen(3))) / safe_s).astype(BF)
    out_s = (self_s2 + mm(mean_s2, wn2[...])).astype(BF)
    flushes = []
    for b in range(blocks):
        span = pl.ds(b * step, step)
        hit = spread[span, :]
        touched = jnp.sum(hit.astype(F32), axis=1, keepdims=True) > 0.0
        outv[span, :] = jnp.where(touched, mm(hit, out_s), outv[span, :].astype(F32)).astype(BF)
        flushes.append(pltpu.make_async_copy(outv.at[span], out_hbm.at[span], out_sem.at[b]))
        flushes[-1].start()
    for phase in range(4):
        wait_bytes(sent.at[phase, others], send_sem.at[phase])
    wait_bytes(sent_n.at[pl.ds(0, number - 1)], n_sem.at[1])
    for flush in flushes:
        flush.wait()


def body(
    features,
    send_rows,
    mirror_count,
    tile_coord,
    tile_mask,
    tile_count,
    w_self1,
    w_neigh1,
    bias1,
    w_self2,
    w_neigh2,
    bias2,
):
    number = lax.axis_size("vert")
    rows, width = features.shape
    slots = send_rows.shape[2]
    _, tiles, block, _ = tile_mask.shape
    mir = number * slots
    size = rows + mir
    flat = mir * (width // LANES)
    pairs = (size // block) ** 2
    wide_links = -(-max(pairs, tiles) // LANES) * LANES
    any_spec = pl.BlockSpec(memory_space=pl.ANY)
    vm = pl.BlockSpec(memory_space=pltpu.VMEM)
    sm = pl.BlockSpec(memory_space=pltpu.SMEM)
    step = 256
    return pl.pallas_call(
        functools.partial(layers_kernel, number, slots, step),
        out_shape=jax.ShapeDtypeStruct((rows, width), BF),
        in_specs=[any_spec, vm, vm, vm, any_spec, sm, any_spec, any_spec, vm, any_spec, any_spec, vm],
        out_specs=any_spec,
        scratch_shapes=[
            pltpu.VMEM((size, width), BF),
            pltpu.VMEM((size, size), BF),
            pltpu.VMEM((tiles, block, block), jnp.int32),
            pltpu.VMEM((tiles + 1, block, block), BF),
            pltpu.VMEM((8, wide_links), jnp.int32),
            pltpu.SMEM((8, wide_links), jnp.int32),
            pltpu.VMEM((width, width), BF),
            pltpu.VMEM((width, width), BF),
            pltpu.VMEM((width, width), BF),
            pltpu.VMEM((width, width), BF),
            pltpu.VMEM((flat, rows), BF),
            pltpu.VMEM((flat, flat), BF),
            pltpu.VMEM((flat, LANES), F32),
            pltpu.VMEM((mir, rows), BF),
            pltpu.VMEM((rows, mir), BF),
            pltpu.VMEM((rows, width), F32),
            pltpu.VMEM((rows, width), F32),
            pltpu.VMEM((rows, LANES), F32),
            pltpu.VMEM((mir, LANES), BF),
            pltpu.VMEM((rows, width), BF),
            pltpu.VMEM((4, flat, LANES), BF),
            pltpu.VMEM((4, flat, LANES), BF),
            pltpu.VMEM((number, 1, mir), F32),
            pltpu.VMEM((number, 1, mir), F32),
            pltpu.SemaphoreType.DMA((5,)),
            pltpu.SemaphoreType.DMA((8,)),
            pltpu.SemaphoreType.DMA,
            pltpu.SemaphoreType.DMA((rows // step,)),
            pltpu.SemaphoreType.DMA((4,)),
            pltpu.SemaphoreType.DMA((4,)),
            pltpu.SemaphoreType.DMA((4,)),
            pltpu.SemaphoreType.DMA((3,)),
        ],
        compiler_params=pltpu.CompilerParams(
            collective_id=0, has_side_effects=True, vmem_limit_bytes=63 * 1024 * 1024
        ),
        name="layers",
    )(
        features,
        jnp.swapaxes(send_rows, 1, 2),
        mirror_count,
        tile_coord,
        tile_mask,
        tile_count,
        w_self1,
        w_neigh1,
        bias1,
        w_self2,
        w_neigh2,
        bias2,
    )


def solution(mesh):
    in_specs = (
        P("vert", None),
        P("vert", None, None),
        P("vert", None),
        P("vert", None, None),
        P("vert", None, None, None),
        P("vert"),
        P(),
        P(),
        P(),
        P(),
        P(),
        P(),
    )
    out_specs = P("vert", None)
    return jax.shard_map(body, mesh=mesh, in_specs=in_specs, out_specs=out_specs, check_vma=False)
```

```python
import functools

import jax
import jax.numpy as jnp
from jax import lax
from jax.experimental import pallas as pl
from jax.experimental.pallas import tpu as pltpu
from jax.sharding import PartitionSpec as P

LANES = 128
DEAD = 64.0
BF = jnp.bfloat16
F32 = jnp.float32


def div(x, n):
    return x >> (n.bit_length() - 1) if n & (n - 1) == 0 else x // n


def mod(x, n):
    return x & (n - 1) if n & (n - 1) == 0 else x % n


def mm(a, b):
    return jnp.dot(a, b, preferred_element_type=F32)


def layers_kernel(
    number,
    slots,
    step,
    feat_hbm,
    send_rows,
    mirror_count,
    coord,
    mask_hbm,
    tile_count,
    ws1_hbm,
    wn1_hbm,
    b1,
    ws2_hbm,
    wn2_hbm,
    b2,
    early_hbm,
    late,
    first_hbm,
    table,
    a,
    held,
    prefix,
    links,
    link_s,
    ws1,
    wn1,
    ws2,
    wn2,
    a_flat,
    a_packed,
    base,
    pick,
    spread,
    acc,
    selfp,
    denom,
    live_m,
    outv,
    sent,
    came,
    sent_n,
    came_n,
    load_sem,
    mask_sem,
    link_sem,
    out_sem,
    send_sem,
    recv_sem,
    own_sem,
    n_sem,
):
    me = lax.axis_index("vert")
    rows, width = feat_hbm.shape
    mir = number * slots
    kb = width // LANES
    chunk = slots * kb
    flat = mir * kb
    size = rows + mir

    barrier = pltpu.get_barrier_semaphore()

    @pl.loop(1, number)
    def _(s):
        pl.semaphore_signal(barrier, inc=1, device_id=(lax.rem(me + s, number),), device_id_type=pl.DeviceIdType.MESH)

    loads = [
        pltpu.make_async_copy(feat_hbm, table.at[pl.ds(0, rows)], load_sem.at[0]),
        pltpu.make_async_copy(ws1_hbm, ws1, load_sem.at[1]),
        pltpu.make_async_copy(wn1_hbm, wn1, load_sem.at[2]),
        pltpu.make_async_copy(ws2_hbm, ws2, load_sem.at[3]),
        pltpu.make_async_copy(wn2_hbm, wn2, load_sem.at[4]),
    ]
    tiles, block = mask_hbm.shape[1], mask_hbm.shape[2]
    groups = mask_sem.shape[0]
    group = tiles // groups
    blocks_a = size // block

    def mask_copy(g):
        span = pl.ds(g * group, group)
        return pltpu.make_async_copy(mask_hbm.at[0, span], held.at[span], mask_sem.at[g])

    loads[0].start()
    for g in range(groups):
        mask_copy(g).start()
    for load in loads[1:]:
        load.start()

    def iota(shape, dim):
        return lax.broadcasted_iota(jnp.int32, shape, dim)

    def one_hot(cond):
        return jnp.where(cond, 1.0, 0.0).astype(BF)

    def column_to_row(col, height):
        return jnp.transpose(jnp.broadcast_to(col, (col.shape[0], height)))[:1, :]

    key_row = (coord[0, :1, :] * blocks_a + coord[0, 1:2, :]).astype(F32)
    key_col = jnp.transpose(jnp.broadcast_to(key_row, (LANES, tiles)))[:, :1].astype(jnp.int32)
    key_row = key_row.astype(jnp.int32)
    place = iota((tiles, tiles), 0)
    before = jnp.where((key_col == key_row) & (place < iota((tiles, tiles), 1)), place + 1, 0)
    wide_links = links.shape[1]
    links[...] = jnp.zeros_like(links)
    links[0:1, pl.ds(0, tiles)] = jnp.max(before, axis=0, keepdims=True)
    spot = iota((tiles, wide_links), 0)
    ended = (key_col == iota((tiles, wide_links), 1)) & (spot < tile_count[0])
    links[1:2, :] = jnp.max(jnp.where(ended, spot + 1, 0), axis=0, keepdims=True)
    to_scalar = pltpu.make_async_copy(links, link_s, link_sem)
    to_scalar.start()

    slot_col = mod(iota((mir, 1), 0), slots)
    expand = one_hot(slot_col == iota((mir, slots), 1))
    raw = send_rows[0]
    each = mm(expand, (div(raw, 256)).astype(F32).astype(BF)) * 256.0 + mm(expand, (mod(raw, 256)).astype(F32).astype(BF))
    peer_hit = iota((mir, number), 1) == div(iota((mir, number), 0), slots)
    row_col = jnp.sum(jnp.where(peer_hit, each, 0.0), axis=1, keepdims=True)
    count_col = jnp.sum(jnp.where(peer_hit, mirror_count[...], 0).astype(F32), axis=1, keepdims=True)
    enc_f = jnp.where(slot_col.astype(F32) < count_col, row_col, -1.0)
    enc_col = enc_f.astype(jnp.int32)
    enc_row = column_to_row(enc_f, LANES).astype(jnp.int32)

    pick[...] = one_hot(iota((mir, rows), 1) == enc_col)
    live_s = enc_col >= 0
    spread[...] = one_hot(iota((rows, mir), 0) == enc_row)
    fr = iota((flat, mir), 0)
    to_flat = one_hot(div(fr, chunk) * slots + mod(fr, slots) == iota((flat, mir), 1))
    fc = iota((mir, flat), 1)
    from_flat = one_hot(div(fc, chunk) * slots + mod(fc, slots) == iota((mir, flat), 0))
    part = div(mod(iota((flat, LANES), 0), chunk), slots)

    def own_lanes(wide):
        total = wide[:, :LANES]
        for k in range(1, kb):
            total = jnp.where(part == k, wide[:, k * LANES : (k + 1) * LANES], total)
        return total

    def pack(phase, value):
        sent[phase] = own_lanes(mm(to_flat, value)).astype(BF)

    def widen(phase):
        narrow = came[phase]
        zero = jnp.zeros_like(narrow)
        return jnp.concatenate([jnp.where(part == k, narrow, zero) for k in range(kb)], axis=1)

    def unpack(phase):
        return mm(from_flat, widen(phase))

    def send(phase):
        pltpu.make_async_copy(
            sent.at[phase, pl.ds(me * chunk, chunk)], came.at[phase, pl.ds(me * chunk, chunk)], own_sem.at[phase]
        ).start()

        @pl.loop(1, number)
        def _(s):
            dst = lax.rem(me + s, number)
            pltpu.make_async_remote_copy(
                src_ref=sent.at[phase, pl.ds(dst * chunk, chunk)],
                dst_ref=came.at[phase, pl.ds(me * chunk, chunk)],
                send_sem=send_sem.at[phase],
                recv_sem=recv_sem.at[phase],
                device_id=(dst,),
                device_id_type=pl.DeviceIdType.MESH,
            ).start()

    def wait_bytes(ref, sem):
        pltpu.make_async_copy(ref, ref, sem).wait()

    others = pl.ds(0, (number - 1) * chunk)

    def arrive(phase):
        pltpu.make_async_copy(
            sent.at[phase, pl.ds(me * chunk, chunk)], came.at[phase, pl.ds(me * chunk, chunk)], own_sem.at[phase]
        ).wait()
        wait_bytes(came.at[phase, others], recv_sem.at[phase])

    blocks = rows // step

    def over_rows(fn):
        @pl.loop(0, blocks)
        def _(b):
            fn(pl.ds(pl.multiple_of(b * step, step), step))

    loads[0].wait()
    gathered = mm(pick[...], table[pl.ds(0, rows), :])
    feat_s = gathered.astype(BF)
    pack(0, jnp.where(live_s, gathered, DEAD).astype(BF))
    pl.semaphore_wait(barrier, number - 1)
    send(0)

    to_scalar.wait()
    prefix[0] = jnp.zeros((block, block), BF)
    for g in range(groups):
        mask_copy(g).wait()

        @pl.loop(g * group, (g + 1) * group, unroll=4)
        def _(t):
            prefix[t + 1] = held[t].astype(F32).astype(BF) + prefix[link_s[0, t]]

    eye = one_hot(iota((block, block), 0) == iota((block, block), 1))
    for b in range(blocks_a):
        for c in range(blocks_a):
            piece = prefix[link_s[1, b * blocks_a + c]]
            if b == c and b < rows // block:
                piece = piece + eye
            a[b * block : (b + 1) * block, c * block : (c + 1) * block] = piece

    a_flat[...] = mm(to_flat, a[pl.ds(rows, mir), pl.ds(0, rows)]).astype(BF)
    base[...] = own_lanes(mm(a_flat[...], table[pl.ds(0, rows), :]))
    a_rep = mm(to_flat, a[pl.ds(rows, mir), pl.ds(rows, mir)]).astype(BF)
    high = flat // 4
    for h in range(4):
        kr = div(mod(iota((high, flat), 0) + h * high, chunk), slots)
        kc = div(mod(iota((high, flat), 1), chunk), slots)
        piece = mm(a_rep[h * high : (h + 1) * high], from_flat)
        a_packed[h * high : (h + 1) * high, :] = jnp.where(kr == kc, piece, 0.0).astype(BF)

    arrive(0)
    fresh = came[0].astype(F32)
    clean = jnp.where(fresh < DEAD / 2, fresh, 0.0).astype(BF)
    sent[1] = (base[...] + mm(a_packed[...], clean)).astype(BF)
    send(1)

    got = unpack(0)
    alive = got[:, :1] < DEAD / 2
    live_m[...] = jnp.broadcast_to(one_hot(alive), (mir, LANES))
    table[pl.ds(rows, mir), :] = jnp.where(alive, got, 0.0).astype(BF)
    ones = jnp.concatenate([jnp.ones((rows, LANES), BF), live_m[...]], axis=0)
    a_m = a[pl.ds(rows, mir), :]
    counted = mm(a_m, ones)[:, :1]
    upper = jnp.floor(counted * (1.0 / 256.0))
    lower = counted - upper * 256.0
    slot_of = mod(iota((mir, mir), 0), slots)
    at_me = iota((mir, mir), 1) == me * slots + slot_of
    by_peer = one_hot(div(iota((number, mir), 1), slots) == iota((number, mir), 0))
    sent_n[:, 0, :] = mm(by_peer, jnp.where(at_me, upper, 0.0).astype(BF)) * 256.0 + mm(
        by_peer, jnp.where(at_me, lower, 0.0).astype(BF)
    )
    own_n = pltpu.make_async_copy(sent_n.at[me], came_n.at[me], n_sem.at[0])
    own_n.start()

    @pl.loop(1, number)
    def _(s):
        dst = lax.rem(me + s, number)
        pltpu.make_async_remote_copy(
            src_ref=sent_n.at[dst],
            dst_ref=came_n.at[me],
            send_sem=n_sem.at[1],
            recv_sem=n_sem.at[2],
            device_id=(dst,),
            device_id_type=pl.DeviceIdType.MESH,
        ).start()

    loads[1].wait()
    self_s = mm(feat_s, ws1[...]) + b1[...].astype(F32)[None, :]
    same = mm(pick[...], spread[...]).astype(BF)
    same_flat = mm(same, from_flat).astype(BF)
    a_s = mm(pick[...], a[pl.ds(0, rows), :]).astype(BF)
    acc_s = mm(a_s, table[...])
    denom_s = mm(a_s, ones)[:, :1]

    def own1(span):
        selfp[span, :] = mm(table[span, :], ws1[...]) + b1[...].astype(F32)[None, :]
        acc[span, :] = mm(a[span, :], table[...])
        denom[span, :] = mm(a[span, :], ones)

    over_rows(own1)
    loads[2].wait()

    own_n.wait()
    wait_bytes(came_n.at[pl.ds(0, number - 1)], n_sem.at[2])
    counts = jnp.sum(came_n[:, 0, :], axis=0, keepdims=True)
    denom_s = denom_s + jnp.sum(same.astype(F32) * counts, axis=1, keepdims=True)

    arrive(1)
    safe_s = jnp.maximum(denom_s, 1.0)
    mean_s = ((acc_s + mm(same_flat, widen(1))) / safe_s).astype(BF)
    hid_s = jnp.maximum(self_s + mm(mean_s, wn1[...]), 0.0)
    pack(2, jnp.where(live_s, hid_s, 0.0).astype(BF))
    send(2)
    ret = unpack(1).astype(BF)

    def hidden(span):
        full = denom[span, :1] + jnp.sum(spread[span, :].astype(F32) * counts, axis=1, keepdims=True)
        denom[span, :] = jnp.broadcast_to(full, (step, LANES))
        mean = ((acc[span, :] + mm(spread[span, :], ret)) / full).astype(BF)
        table[span, :] = jnp.maximum(selfp[span, :] + mm(mean, wn1[...]), 0.0).astype(BF)

    over_rows(hidden)
    base[...] = own_lanes(mm(a_flat[...], table[pl.ds(0, rows), :]))
    loads[3].wait()

    def self2(span):
        selfp[span, :] = mm(table[span, :], ws2[...]) + b2[...].astype(F32)[None, :]

    over_rows(self2)

    def own2(span):
        acc[span, :] = mm(a[span, pl.ds(0, rows)], table[pl.ds(0, rows), :])

    over_rows(own2)
    loads[4].wait()

    arrive(2)
    sent[3] = (base[...] + mm(a_packed[...], came[2])).astype(BF)
    send(3)
    table[pl.ds(rows, mir), :] = unpack(2).astype(BF)

    def early(span):
        total = acc[span, :] + mm(a[span, pl.ds(rows, mir)], table[pl.ds(rows, mir), :])
        mean = (total / denom[span, :1]).astype(BF)
        outv[span, :] = (selfp[span, :] + mm(mean, wn2[...])).astype(BF)

    over_rows(early)
    acc_s2 = mm(a_s, table[...])
    self_s2 = mm(hid_s.astype(BF), ws2[...]) + b2[...].astype(F32)[None, :]
    earlier = iota((mir, mir), 0) < iota((mir, mir), 1)
    again = jnp.max(jnp.where(earlier, same.astype(F32), 0.0), axis=0, keepdims=True)

    def firsts(span):
        spread[span, :] = jnp.where(again > 0.0, 0.0, spread[span, :].astype(F32)).astype(BF)

    over_rows(firsts)
    flushes = [
        pltpu.make_async_copy(outv, early_hbm, out_sem.at[0]),
        pltpu.make_async_copy(spread, first_hbm, out_sem.at[1]),
    ]
    for flush in flushes:
        flush.start()
    arrive(3)
    mean_s2 = ((acc_s2 + mm(same_flat, widen(3))) / safe_s).astype(BF)
    late[...] = (self_s2 + mm(mean_s2, wn2[...])).astype(BF)
    for phase in range(4):
        wait_bytes(sent.at[phase, others], send_sem.at[phase])
    wait_bytes(sent_n.at[pl.ds(0, number - 1)], n_sem.at[1])
    for flush in flushes:
        flush.wait()


def select_kernel(early, late, first, out):
    hit = first[...]
    touched = jnp.sum(hit.astype(F32), axis=1, keepdims=True) > 0.0
    out[...] = jnp.where(touched, mm(hit, late[...]), early[...].astype(F32)).astype(BF)


def body(
    features,
    send_rows,
    mirror_count,
    tile_coord,
    tile_mask,
    tile_count,
    w_self1,
    w_neigh1,
    bias1,
    w_self2,
    w_neigh2,
    bias2,
):
    number = lax.axis_size("vert")
    rows, width = features.shape
    slots = send_rows.shape[2]
    _, tiles, block, _ = tile_mask.shape
    mir = number * slots
    size = rows + mir
    flat = mir * (width // LANES)
    pairs = (size // block) ** 2
    wide_links = -(-max(pairs, tiles) // LANES) * LANES
    any_spec = pl.BlockSpec(memory_space=pl.ANY)
    vm = pl.BlockSpec(memory_space=pltpu.VMEM)
    sm = pl.BlockSpec(memory_space=pltpu.SMEM)
    step = 256
    early, late, first = pl.pallas_call(
        functools.partial(layers_kernel, number, slots, step),
        out_shape=(
            jax.ShapeDtypeStruct((rows, width), BF),
            jax.ShapeDtypeStruct((mir, width), BF),
            jax.ShapeDtypeStruct((rows, mir), BF),
        ),
        in_specs=[any_spec, vm, vm, vm, any_spec, sm, any_spec, any_spec, vm, any_spec, any_spec, vm],
        out_specs=(any_spec, vm, any_spec),
        scratch_shapes=[
            pltpu.VMEM((size, width), BF),
            pltpu.VMEM((size, size), BF),
            pltpu.VMEM((tiles, block, block), jnp.int32),
            pltpu.VMEM((tiles + 1, block, block), BF),
            pltpu.VMEM((8, wide_links), jnp.int32),
            pltpu.SMEM((8, wide_links), jnp.int32),
            pltpu.VMEM((width, width), BF),
            pltpu.VMEM((width, width), BF),
            pltpu.VMEM((width, width), BF),
            pltpu.VMEM((width, width), BF),
            pltpu.VMEM((flat, rows), BF),
            pltpu.VMEM((flat, flat), BF),
            pltpu.VMEM((flat, LANES), F32),
            pltpu.VMEM((mir, rows), BF),
            pltpu.VMEM((rows, mir), BF),
            pltpu.VMEM((rows, width), F32),
            pltpu.VMEM((rows, width), F32),
            pltpu.VMEM((rows, LANES), F32),
            pltpu.VMEM((mir, LANES), BF),
            pltpu.VMEM((rows, width), BF),
            pltpu.VMEM((4, flat, LANES), BF),
            pltpu.VMEM((4, flat, LANES), BF),
            pltpu.VMEM((number, 1, mir), F32),
            pltpu.VMEM((number, 1, mir), F32),
            pltpu.SemaphoreType.DMA((5,)),
            pltpu.SemaphoreType.DMA((8,)),
            pltpu.SemaphoreType.DMA,
            pltpu.SemaphoreType.DMA((2,)),
            pltpu.SemaphoreType.DMA((4,)),
            pltpu.SemaphoreType.DMA((4,)),
            pltpu.SemaphoreType.DMA((4,)),
            pltpu.SemaphoreType.DMA((3,)),
        ],
        compiler_params=pltpu.CompilerParams(
            collective_id=0, has_side_effects=True, vmem_limit_bytes=63 * 1024 * 1024
        ),
        name="layers",
    )(
        features,
        jnp.swapaxes(send_rows, 1, 2),
        mirror_count,
        tile_coord,
        tile_mask,
        tile_count,
        w_self1,
        w_neigh1,
        bias1,
        w_self2,
        w_neigh2,
        bias2,
    )
    tall = rows // 2
    return pl.pallas_call(
        select_kernel,
        grid=(rows // tall,),
        out_shape=jax.ShapeDtypeStruct((rows, width), BF),
        in_specs=[
            pl.BlockSpec((tall, width), lambda b: (b, 0)),
            pl.BlockSpec((mir, width), lambda b: (0, 0)),
            pl.BlockSpec((tall, mir), lambda b: (b, 0)),
        ],
        out_specs=pl.BlockSpec((tall, width), lambda b: (b, 0)),
        compiler_params=pltpu.CompilerParams(vmem_limit_bytes=62 * 1024 * 1024),
        name="select",
    )(early, late, first)


def solution(mesh):
    in_specs = (
        P("vert", None),
        P("vert", None, None),
        P("vert", None),
        P("vert", None, None),
        P("vert", None, None, None),
        P("vert"),
        P(),
        P(),
        P(),
        P(),
        P(),
        P(),
    )
    out_specs = P("vert", None)
    return jax.shard_map(body, mesh=mesh, in_specs=in_specs, out_specs=out_specs, check_vma=False)
```
